1024 devices in a mesh: dp: 16 (over z), fsdp: 4 (over x), expert: 16 (over y, core).
Axes of the slice: x: 4, y: 8, z: 16, core: 2. Of those that a mesh axis runs over, the one named last changes fastest.
Arguments:
- tokens: bfloat16 [32768, 4096], P(('dp', 'expert'), 'fsdp'), may hold values from -24 to 24
- cotangent: bfloat16 [32768, 4096], P(('dp', 'expert'), 'fsdp'), may hold values from -6 to 6
- routes: int32 [32768, 8], P(('dp', 'expert')), may hold values from 0 to 127, as said below
- route_gates: float32 [32768, 8], P(('dp', 'expert')), may hold values from 0.05 to 0.6
- gate_weight: bfloat16 [16, 4096, 768], P('expert', None, 'fsdp'), may hold values from -0.09375 to 0.09375
- up_weight: bfloat16 [16, 4096, 768], P('expert', None, 'fsdp'), may hold values from -0.09375 to 0.09375
- down_weight: bfloat16 [16, 768, 4096], P('expert', 'fsdp'), may hold values from -0.21875 to 0.21875
Outputs:
- token_grads: bfloat16 [32768, 4096], P(('dp', 'expert'), 'fsdp')
- gate_grads: bfloat16 [16, 4096, 768], P('expert', 'dp', 'fsdp')
- up_grads: bfloat16 [16, 4096, 768], P('expert', 'dp', 'fsdp')
- down_grads: bfloat16 [16, 768, 4096], P('expert', 'fsdp', 'dp')
The draws below stay inside these ranges and needn't reach their ends.
Inputs may be any that keep to these rules, and one draw needn't show every extreme that they name: `routes`: each token names 8 different ids, exactly one in each run of 16 ids (0 to 15, 16 to 31, and so on). In each aligned block of 128 tokens (one index of dp and expert together) no id below 16 is named by more than 10 tokens, and in every draw one id below 16 is named by exactly 10 tokens of every block.
All inputs are finite; a program needn't handle non-finite values.
Results may differ from the reference program's by a relative error of at most 0.017.
Values may be sent and summed in bfloat16 or wider, within the bound.
No kernel may reach another device: no remote copies, remote signals or barrier semaphores. Data moves between devices by JAX's collectives and lax.ppermute only.
A program may use at most 32 MiB of HBM per device.

```python
import jax
import jax.numpy as jnp
from jax import lax

D = 4096
TOPK = 8
FF_WIN = 768
TOK = 128
GROUP = 16
CAP = 10
EXPERTS = 16
TOKENS = 32768
N_DP = 16
N_FSDP = 4
N_EXPERT = 16


def draw_routes(key, part):
    keys = jax.random.split(key, 4)
    favored = jax.random.randint(keys[0], (), 0, EXPERTS)
    pooled = ((jnp.arange(GROUP * CAP, dtype=jnp.int32) // CAP + favored) % GROUP).astype(jnp.int32)

    def one_block(block_key):
        first_key, second_key = jax.random.split(block_key)
        others = jax.random.permutation(first_key, pooled[CAP:])
        chosen = jnp.concatenate([pooled[:CAP], others[:TOK - CAP]])
        return jax.random.permutation(second_key, chosen)
    window_ids = jax.vmap(one_block)(jax.random.split(keys[1], TOKENS // TOK)).reshape(TOKENS)
    spare = jax.random.randint(keys[2], (TOKENS, TOPK), 0, GROUP)
    scores = jax.random.randint(keys[3], (TOKENS, TOPK), 0, 1048576) * TOPK + jnp.arange(TOPK, dtype=jnp.int32)[None, :]
    groups = jnp.argsort(scores, axis=1).astype(jnp.int32)
    local_ids = jnp.where(groups == 0, window_ids[:, None], spare)
    return (groups * GROUP + local_ids).astype(jnp.int32)


def raised(array, stream_key, source, target, shards_of, factor):
    def block_of(position):
        return (jnp.arange(array.shape[position]) // (array.shape[position] // shards_of)).reshape((-1,) + (1,) * (array.ndim - 1 - position))

    one_side = jax.random.permutation(stream_key, shards_of)[block_of(target)]
    second = (block_of(target) + shards_of // 2) % shards_of
    return jnp.where((block_of(source) == one_side) | (block_of(source) == second), factor * array, array)


def levels(own_key, dims, pieces, least, high):
    gain, own = 1.0, jax.random.fold_in(own_key, 6)
    for position, shards_of in pieces:
        heights = jnp.exp(jax.random.uniform(jax.random.fold_in(own, position), (shards_of,), jnp.float32, least / len(pieces), high / len(pieces)))
        gain = gain * jnp.repeat(heights, dims[position] // shards_of).reshape([-1 if axis == position else 1 for axis in range(len(dims))])
    return gain


def bell_draw(stream_key, dims, deviation, most, shards=(), kind=jnp.bfloat16):
    values = jax.random.normal(stream_key, dims, jnp.float32) * deviation
    if len(shards) > 0:
        values = levels(stream_key, dims, shards, -0.22, 0.18) * values
    return jnp.clip(values, min=-most, max=most).astype(kind)


def bell_draw_with(rng, dims, deviation, limit, pieces, heavy, kind=jnp.bfloat16):
    array = deviation * jax.random.normal(rng, dims, jnp.float32)
    if pieces:
        array = array * levels(rng, dims, pieces, -0.22, 0.18)
    return jnp.clip(raised(array, jax.random.fold_in(rng, 3), *heavy), -limit, limit).astype(kind)


def setup_inputs(seed: int = 0) -> dict:
    streams_of = jax.random.split(jax.random.key(seed), 8)
    tokens = bell_draw_with(streams_of[0], (TOKENS, D), 1.0, 24.0, ((0, 256), (1, 4)), (0, 1, 256, 6.0))
    cotangent = bell_draw(streams_of[1], (TOKENS, D), 1.0, 6.0, ((0, 256), (1, 4)))
    routes = draw_routes(jax.random.fold_in(streams_of[7], 71), 0)
    route_gates = jnp.clip(0.05 + 0.55 * jax.random.uniform(streams_of[3], (TOKENS, TOPK), jnp.float32) ** levels(streams_of[3], (TOKENS, TOPK), ((0, 256),), -0.2, 0.2), 0.05, 0.6)
    gate_weight = bell_draw(streams_of[4], (EXPERTS, D, FF_WIN), D ** -0.5, 0.09375, ((0, 16), (2, 4)))
    up_weight = bell_draw(streams_of[5], (EXPERTS, D, FF_WIN), D ** -0.5, 0.09375, ((0, 16), (2, 4)))
    down_weight = bell_draw(streams_of[6], (EXPERTS, FF_WIN, D), FF_WIN ** -0.5, 0.21875, ((0, 16), (1, 4)))
    return {"tokens": tokens, "cotangent": cotangent, "routes": routes, "route_gates": route_gates, "gate_weight": gate_weight, "up_weight": up_weight, "down_weight": down_weight}


def reference(tokens, cotangent, routes, route_gates, gate_weight, up_weight, down_weight):
    in_window = routes < EXPERTS
    target = jnp.where(jnp.any(in_window, axis=1), jnp.sum(jnp.where(in_window, routes, 0), axis=1), EXPERTS).astype(jnp.int32)
    route_gate = jnp.sum(jnp.where(in_window, route_gates, jnp.float32(0.0)), axis=1)
    scaled = (route_gate[:, None] * cotangent.astype(jnp.float32)).astype(jnp.bfloat16)
    group_rows = TOK * N_EXPERT
    slot_count = CAP * N_EXPERT
    block_width = FF_WIN // N_FSDP
    padding = jnp.zeros((1, D), jnp.bfloat16)
    grouped_rows = tokens.reshape(N_DP, group_rows, D)
    grouped_grads = scaled.reshape(N_DP, group_rows, D)
    grouped_target = target.reshape(N_DP, group_rows)

    def per_expert(expert_id):
        gate_mat = gate_weight[expert_id]
        up_mat = up_weight[expert_id]
        down_mat = down_weight[expert_id]

        def per_group(running, group_id):
            row_index = jnp.nonzero(grouped_target[group_id] == expert_id, size=slot_count, fill_value=group_rows)[0].astype(jnp.int32)
            rows_in = jnp.concatenate([grouped_rows[group_id], padding], axis=0)[row_index]
            grads_in = jnp.concatenate([grouped_grads[group_id], padding], axis=0)[row_index]
            gate_pre = jnp.dot(rows_in, gate_mat, preferred_element_type=jnp.float32)
            up_pre = jnp.dot(rows_in, up_mat, preferred_element_type=jnp.float32)
            sigmoid_gate = jax.nn.sigmoid(gate_pre)
            activated = gate_pre * sigmoid_gate
            hidden = (activated * up_pre).astype(jnp.bfloat16)
            hidden_grad = jnp.dot(grads_in, down_mat.T, preferred_element_type=jnp.float32)
            gate_grad = (hidden_grad * up_pre * sigmoid_gate * (1.0 + gate_pre * (1.0 - sigmoid_gate))).astype(jnp.bfloat16)
            up_grad = (hidden_grad * activated).astype(jnp.bfloat16)
            row_sum = jnp.zeros((slot_count, D), jnp.float32)
            for column_block in range(N_FSDP):
                column_low = column_block * block_width
                column_high = column_low + block_width
                block_term = jnp.dot(gate_grad[:, column_low:column_high], gate_mat[:, column_low:column_high].T, preferred_element_type=jnp.float32)
                block_term = block_term + jnp.dot(up_grad[:, column_low:column_high], up_mat[:, column_low:column_high].T, preferred_element_type=jnp.float32)
                rounded = lax.optimization_barrier(block_term.astype(jnp.bfloat16))
                row_sum = row_sum + rounded.astype(jnp.float32)
            term_gate = jnp.dot(rows_in.T, gate_grad, preferred_element_type=jnp.float32).astype(jnp.bfloat16)
            term_up = jnp.dot(rows_in.T, up_grad, preferred_element_type=jnp.float32).astype(jnp.bfloat16)
            term_down = jnp.dot(hidden.T, grads_in, preferred_element_type=jnp.float32).astype(jnp.bfloat16)
            term_gate, term_up, term_down = lax.optimization_barrier((term_gate, term_up, term_down))
            running = (running[0] + term_gate.astype(jnp.float32), running[1] + term_up.astype(jnp.float32), running[2] + term_down.astype(jnp.float32))
            row_place = jnp.where(row_index < group_rows, row_index + group_id * group_rows, TOKENS).astype(jnp.int32)
            return running, (row_sum.astype(jnp.bfloat16), row_place)

        initial = (jnp.zeros((D, FF_WIN), jnp.float32), jnp.zeros((D, FF_WIN), jnp.float32), jnp.zeros((FF_WIN, D), jnp.float32))
        running, outputs = lax.scan(per_group, initial, jnp.arange(N_DP, dtype=jnp.int32))
        return running[0].astype(jnp.bfloat16), running[1].astype(jnp.bfloat16), running[2].astype(jnp.bfloat16), outputs[0], outputs[1]

    gate_grads, up_grads, down_grads, rows_out, places = lax.map(per_expert, jnp.arange(EXPERTS, dtype=jnp.int32))
    token_grads = jnp.zeros((TOKENS, D), jnp.bfloat16).at[places.reshape(-1)].set(rows_out.reshape(-1, D), mode="drop")
    return token_grads, gate_grads, up_grads, down_grads
```

```python
import jax
import jax.numpy as jnp
from jax import lax
from jax.sharding import PartitionSpec as P

CAP = 10
MAIN = 8
TAIL = CAP - MAIN


def packed(values, main_pick, tail_picks):
    pieces = len(tail_picks)
    width = values.shape[1] // pieces
    main = jnp.dot(main_pick, values, preferred_element_type=jnp.float32)
    stacked = jnp.concatenate([values[:, p * width : (p + 1) * width] for p in range(pieces)], 0)
    tail = jnp.dot(
        jnp.concatenate(tail_picks, axis=1), stacked, preferred_element_type=jnp.float32
    )
    return jnp.concatenate([main.astype(jnp.bfloat16), tail.astype(jnp.bfloat16)], axis=1)


def unpacked(received, quarter):
    owners = received.shape[0]
    main = received[:, :, :quarter].reshape(owners * MAIN, quarter)
    tail = received[:, :, quarter:].reshape(owners * TAIL, quarter)
    return jnp.concatenate([main, tail], axis=0)


def local(tokens, cotangent, routes, route_gates, gate_weight, up_weight, down_weight):
    owners = lax.axis_size("expert")
    quarters = lax.axis_size("fsdp")
    quarter = tokens.shape[1]
    pieces = MAIN // TAIL
    in_window = routes < owners
    target = jnp.sum(jnp.where(in_window, routes, 0), axis=1)
    route_gate = jnp.sum(jnp.where(in_window, route_gates, jnp.float32(0.0)), axis=1)
    scaled = (route_gate[:, None] * cotangent.astype(jnp.float32)).astype(jnp.bfloat16)
    onehot = (target[:, None] == jnp.arange(owners, dtype=jnp.int32)[None, :]).astype(jnp.bfloat16)
    count = tokens.shape[0]
    earlier = (
        jnp.arange(count)[:, None] > jnp.arange(count)[None, :]
    ).astype(jnp.bfloat16)
    before = jnp.dot(earlier, onehot, preferred_element_type=jnp.float32)
    rank = jnp.sum(before * onehot.astype(jnp.float32), axis=1).astype(jnp.int32)
    row = jnp.arange(owners * MAIN, dtype=jnp.int32)[:, None]
    owner_row, place = row // MAIN, row % MAIN
    to_owner = owner_row == target[None, :]
    main_pick = (to_owner & (place == rank[None, :])).astype(jnp.bfloat16)
    in_tail = to_owner & (place // pieces + MAIN == rank[None, :])
    tail_picks = [(in_tail & (place % pieces == p)).astype(jnp.bfloat16) for p in range(pieces)]
    shape = (owners, MAIN, quarter + quarter // pieces)
    send_rows = packed(tokens, main_pick, tail_picks).reshape(shape)
    recv_rows = lax.all_to_all(send_rows, "expert", split_axis=0, concat_axis=0, tiled=True)
    send_grads = packed(scaled, main_pick, tail_picks).reshape(shape)
    recv_rows, send_grads = lax.optimization_barrier((recv_rows, send_grads))
    recv_grads = lax.all_to_all(send_grads, "expert", split_axis=0, concat_axis=0, tiled=True)
    full_rows = lax.all_gather(unpacked(recv_rows, quarter), "fsdp", axis=1, tiled=True)
    flat_grads = unpacked(recv_grads, quarter)
    slot_count = flat_grads.shape[0]
    grad_blocks = lax.all_to_all(
        jnp.broadcast_to(flat_grads[None], (quarters, slot_count, quarter)),
        "fsdp",
        split_axis=0,
        concat_axis=0,
        tiled=True,
    )
    full_grads = jnp.concatenate([grad_blocks[k] for k in range(quarters)], axis=1)
    gate_mat = gate_weight[0]
    up_mat = up_weight[0]
    down_mat = down_weight[0]
    across = (((1,), (1,)), ((), ()))
    gate_pre = jnp.dot(full_rows, gate_mat, preferred_element_type=jnp.float32)
    up_pre = jnp.dot(full_rows, up_mat, preferred_element_type=jnp.float32)
    sigmoid_gate = jax.nn.sigmoid(gate_pre)
    activated = gate_pre * sigmoid_gate
    hidden = (activated * up_pre).astype(jnp.bfloat16)
    hidden_grad = lax.dot_general(full_grads, down_mat, across, preferred_element_type=jnp.float32)
    gate_grad = (
        hidden_grad * up_pre * sigmoid_gate * (1.0 + gate_pre * (1.0 - sigmoid_gate))
    ).astype(jnp.bfloat16)
    up_grad = (hidden_grad * activated).astype(jnp.bfloat16)
    contract = (((0,), (0,)), ((), ()))
    gate_up = jnp.concatenate([gate_grad, up_grad], axis=1)
    term_gate_up = lax.dot_general(gate_up, full_rows, contract, preferred_element_type=jnp.float32)
    term_down = lax.dot_general(hidden, full_grads, contract, preferred_element_type=jnp.float32)
    terms = jnp.concatenate(
        [term_gate_up.astype(jnp.bfloat16), term_down.astype(jnp.bfloat16)], axis=0
    )
    sums = lax.psum_scatter(terms, "dp", scatter_dimension=1, tiled=True)
    partial_value = lax.dot_general(gate_grad, gate_mat, across, preferred_element_type=jnp.float32)
    partial_value = partial_value + lax.dot_general(
        up_grad, up_mat, across, preferred_element_type=jnp.float32
    )
    blocks = partial_value.astype(jnp.bfloat16)
    blocks = jnp.stack([blocks[:, k * quarter : (k + 1) * quarter] for k in range(quarters)])
    given = lax.all_to_all(blocks, "fsdp", split_axis=0, concat_axis=0, tiled=True)
    route_rows = (
        given[0].astype(jnp.float32)
        + given[1].astype(jnp.float32)
        + given[2].astype(jnp.float32)
        + given[3].astype(jnp.float32)
    ).astype(jnp.bfloat16)
    mains = owners * MAIN
    returned = lax.all_to_all(
        jnp.concatenate(
            [
                route_rows[:mains].reshape(owners, MAIN, quarter),
                route_rows[mains:].reshape(owners, TAIL, quarter),
            ],
            axis=1,
        ),
        "expert",
        split_axis=0,
        concat_axis=0,
        tiled=True,
    )
    slot = jnp.arange(slot_count, dtype=jnp.int32)[None, :]
    selector = (slot == (target * CAP + rank)[:, None]).astype(jnp.bfloat16)
    token_grads = jnp.dot(
        selector, returned.reshape(slot_count, quarter), preferred_element_type=jnp.float32
    ).astype(jnp.bfloat16)
    width = gate_mat.shape[1]
    return (
        token_grads,
        sums[:width].T[None],
        sums[width : 2 * width].T[None],
        sums[2 * width :][None],
    )


def solution(mesh):
    placed = (
        P(("dp", "expert"), "fsdp"),
        P(("dp", "expert"), "fsdp"),
        P(("dp", "expert"), None),
        P(("dp", "expert"), None),
        P("expert", None, "fsdp"),
        P("expert", None, "fsdp"),
        P("expert", "fsdp", None),
    )
    return jax.shard_map(
        local,
        mesh=mesh,
        in_specs=placed,
        out_specs=(
            P(("dp", "expert"), "fsdp"),
            P("expert", "dp", "fsdp"),
            P("expert", "dp", "fsdp"),
            P("expert", "fsdp", "dp"),
        ),
        check_vma=False,
    )
```

```python
import jax
import jax.numpy as jnp
from jax import lax
from jax.experimental import pallas as pl
from jax.experimental.pallas import tpu as pltpu
from jax.sharding import PartitionSpec as P

CAP = 10
MAIN = 8
TAIL = CAP - MAIN
PIECES = MAIN // TAIL
F32 = jnp.float32
BF16 = jnp.bfloat16
NN = (((1,), (0,)), ((), ()))
NT = (((1,), (1,)), ((), ()))
TN = (((0,), (0,)), ((), ()))


def dot(a, b, dims=NN):
    return lax.dot_general(a, b, dims, preferred_element_type=F32)


def iota(shape, axis):
    return lax.broadcasted_iota(jnp.int32, shape, axis)


def places(routes, owners):
    count = routes.shape[1]
    target = jnp.sum(jnp.where(routes < owners, routes, 0), axis=0, keepdims=True)
    mine = iota((owners, count), 0) == target
    earlier = (iota((count, count), 0) < iota((count, count), 1)).astype(BF16)
    before = dot(mine.astype(BF16), earlier)
    rank = jnp.sum(jnp.where(mine, before, 0.0), axis=0, keepdims=True).astype(jnp.int32)
    return target, rank


def send_kernel(
    owners, routes_hbm, gates_hbm, tokens_hbm, cotangent_hbm, out_ref, slot_ref,
    routes_ref, gates_ref, tokens_ref, cotangent_ref, sems,
):
    fetches = [
        pltpu.make_async_copy(source, near, sems.at[i])
        for i, (source, near) in enumerate(
            (
                (routes_hbm, routes_ref),
                (gates_hbm, gates_ref),
                (cotangent_hbm, cotangent_ref),
                (tokens_hbm, tokens_ref),
            )
        )
    ]
    for fetch in fetches:
        fetch.start()
    fetches[0].wait()
    routes = routes_ref[...]
    target, rank = places(routes, owners)
    slot_ref[...] = jnp.broadcast_to(target * CAP + rank, slot_ref.shape)
    fetches[1].wait()
    gate = jnp.where(routes < owners, gates_ref[...], 0.0)
    gate = jnp.sum(jnp.transpose(gate), axis=1, keepdims=True)
    fetches[2].wait()
    scaled = (gate * cotangent_ref[...].astype(F32)).astype(BF16)
    fetches[3].wait()
    values = jnp.concatenate([tokens_ref[...], scaled], axis=0)
    count, quarter = values.shape
    width = quarter // PIECES
    rows = owners * 2 * MAIN
    row, column = iota((rows, count), 0), iota((rows, count), 1)
    target = jnp.concatenate([target, target], axis=1)
    rank = jnp.concatenate([rank, rank], axis=1)
    place = row % MAIN
    wanted = (row // (2 * MAIN) == target) & (row // MAIN % 2 == column // (count // 2))
    main_pick = (wanted & (place == rank)).astype(BF16)
    out_ref[:, :quarter] = dot(main_pick, values).astype(BF16)
    in_tail = wanted & (place // PIECES + MAIN == rank)
    tail = jnp.zeros((rows, width), F32)
    for p in range(PIECES):
        pick = (in_tail & (place % PIECES == p)).astype(BF16)
        tail = tail + dot(pick, values[:, p * width : (p + 1) * width])
    out_ref[:, quarter:] = tail.astype(BF16)


def tail_pick(rows, p):
    tails = rows // MAIN * TAIL
    slot, row = iota((tails, rows), 0), iota((tails, rows), 1)
    return (row == slot // TAIL * MAIN + slot % TAIL * PIECES + p).astype(BF16)


def forward_kernel(rows_ref, gate_ref, up_ref, full_hbm, mid_hbm, full_ref, mid_ref, sems):
    quarters, mains, _ = rows_ref.shape
    quarter = full_ref.shape[1] // quarters
    width = quarter // PIECES
    wide = gate_ref.shape[0]
    picks = [tail_pick(mains, p) for p in range(PIECES)]
    for j in range(quarters):
        low = j * quarter
        full_ref[:mains, low : low + quarter] = rows_ref[j, :, :quarter]
        packed = rows_ref[j, :, quarter:]
        for p in range(PIECES):
            start = low + p * width
            full_ref[mains:, start : start + width] = dot(picks[p], packed).astype(BF16)
    keep_full = pltpu.make_async_copy(full_ref, full_hbm, sems.at[0])
    keep_full.start()
    gate_pre = jnp.zeros((wide, full_ref.shape[0]), F32)
    up_pre = jnp.zeros((wide, full_ref.shape[0]), F32)
    for j in range(quarters):
        low = j * quarter
        block = full_ref[:, low : low + quarter]
        gate_pre = gate_pre + dot(gate_ref[:, low : low + quarter], block, NT)
        up_pre = up_pre + dot(up_ref[:, low : low + quarter], block, NT)
    sigmoid_gate = jax.nn.sigmoid(gate_pre)
    activated = gate_pre * sigmoid_gate
    mid_ref[:wide, :] = up_pre * sigmoid_gate * (1.0 + gate_pre * (1.0 - sigmoid_gate))
    mid_ref[wide : 2 * wide, :] = activated
    mid_ref[2 * wide :, :] = activated * up_pre
    keep_mid = pltpu.make_async_copy(mid_ref, mid_hbm, sems.at[1])
    keep_mid.start()
    keep_full.wait()
    keep_mid.wait()


def backward_kernel(
    grads_hbm, down_hbm, full_hbm, mid_hbm, terms_hbm, pair_hbm,
    grads_ref, down_ref, full_ref, mid_ref, pair_ref, block_ref, tails_ref, sems,
):
    quarters, mains, _ = grads_ref.shape
    quarter = full_ref.shape[1] // quarters
    width = quarter // PIECES
    wide = down_ref.shape[0]

    def columns(ref, j):
        return ref.at[:, j * quarter : (j + 1) * quarter]

    grads_in = [
        pltpu.make_async_copy(grads_hbm.at[j], grads_ref.at[j], sems.at[0, j])
        for j in range(quarters)
    ]
    down_in = [
        pltpu.make_async_copy(columns(down_hbm, j), columns(down_ref, j), sems.at[1, j])
        for j in range(quarters)
    ]
    full_in = [
        pltpu.make_async_copy(columns(full_hbm, j), columns(full_ref, j), sems.at[2, j])
        for j in range(quarters)
    ]
    mid_in = pltpu.make_async_copy(mid_hbm, mid_ref, sems.at[4, 0])
    for j in range(quarters):
        grads_in[j].start()
        down_in[j].start()
    mid_in.start()
    for j in range(quarters):
        full_in[j].start()
    picks = [tail_pick(mains, p) for p in range(PIECES)]
    main_grad = jnp.zeros((wide, mains), F32)
    tail_grad = jnp.zeros((wide, full_ref.shape[0] - mains), F32)
    for j in range(quarters):
        low = j * quarter
        grads_in[j].wait()
        packed = grads_ref[j, :, quarter:]
        for p in range(PIECES):
            start = low + p * width
            tails_ref[:, start : start + width] = dot(picks[p], packed).astype(BF16)
        down_in[j].wait()
        weight = down_ref[:, low : low + quarter]
        main_grad = main_grad + dot(weight, grads_ref[j, :, :quarter], NT)
        tail_grad = tail_grad + dot(weight, tails_ref[:, low : low + quarter], NT)
    hidden_grad = jnp.concatenate([main_grad, tail_grad], axis=1)
    mid_in.wait()
    pair_ref[:wide, :] = (hidden_grad * mid_ref[:wide, :]).astype(BF16)
    pair_ref[wide:, :] = (hidden_grad * mid_ref[wide : 2 * wide, :]).astype(BF16)
    hidden = mid_ref[2 * wide :, :].astype(BF16)
    outs = [pltpu.make_async_copy(pair_ref, pair_hbm, sems.at[4, 1])]
    outs[0].start()
    for j in range(quarters):
        low = j * quarter
        full_in[j].wait()
        block_ref[j, : 2 * wide, :] = dot(
            pair_ref[...], full_ref[:, low : low + quarter]
        ).astype(BF16)
        down_term = dot(hidden[:, :mains], grads_ref[j, :, :quarter])
        down_term = down_term + dot(hidden[:, mains:], tails_ref[:, low : low + quarter])
        block_ref[j, 2 * wide :, :] = down_term.astype(BF16)
        out = pltpu.make_async_copy(block_ref.at[j], columns(terms_hbm, j), sems.at[3, j])
        out.start()
        outs.append(out)
    for out in outs:
        out.wait()


def vmem():
    return pl.BlockSpec(memory_space=pltpu.VMEM)


def hbm():
    return pl.BlockSpec(memory_space=pltpu.HBM)


def far(*arrays):
    return [pltpu.with_memory_space_constraint(x, pltpu.HBM) for x in arrays]


def call(kernel, operands, outs, name, limit_mib, in_specs=None, out_specs=None, scratch=()):
    return pl.pallas_call(
        kernel,
        out_shape=outs,
        in_specs=in_specs if in_specs is not None else [vmem() for _ in operands],
        out_specs=out_specs if out_specs is not None else [vmem() for _ in outs],
        scratch_shapes=scratch,
        compiler_params=pltpu.CompilerParams(vmem_limit_bytes=limit_mib * 1024 * 1024),
        name=name,
    )(*operands)


def local(tokens, cotangent, routes, route_gates, gate_weight, up_weight, down_weight):
    owners = lax.axis_size("expert")
    quarters = lax.axis_size("fsdp")
    count, quarter = tokens.shape
    model = quarter * quarters
    mains = owners * MAIN
    slots = owners * CAP
    packed_width = quarter + quarter // PIECES

    def to_owners(x):
        return lax.all_to_all(x, "expert", split_axis=0, concat_axis=0, tiled=True)

    def to_quarters(x):
        return lax.all_to_all(x, "fsdp", split_axis=0, concat_axis=0, tiled=True)

    sent, slot = call(
        lambda *refs: send_kernel(owners, *refs),
        far(routes.T, route_gates.T, tokens, cotangent),
        (
            jax.ShapeDtypeStruct((2 * mains, packed_width), BF16),
            jax.ShapeDtypeStruct((8, count), jnp.int32),
        ),
        "send",
        8,
        in_specs=[hbm()] * 4,
        scratch=[
            pltpu.VMEM(routes.shape[::-1], jnp.int32),
            pltpu.VMEM(route_gates.shape[::-1], F32),
            pltpu.VMEM(tokens.shape, BF16),
            pltpu.VMEM(cotangent.shape, BF16),
            pltpu.SemaphoreType.DMA((4,)),
        ],
    )
    received = to_owners(sent.reshape(owners, 2 * MAIN, packed_width))
    recv_rows = received[:, :MAIN].reshape(mains, packed_width)
    recv_grads = received[:, MAIN:].reshape(mains, packed_width)
    grads4 = lax.all_gather(recv_grads, "fsdp", axis=0, tiled=True)
    grads4 = grads4.reshape(quarters, mains, packed_width)
    rows4 = to_quarters(jnp.broadcast_to(recv_rows[None], (quarters, mains, packed_width)))
    gate_mat = jnp.swapaxes(gate_weight, 1, 2)[0]
    up_mat = jnp.swapaxes(up_weight, 1, 2)[0]
    down_mat = down_weight[0]
    width = gate_mat.shape[0]
    full_rows, mid = call(
        forward_kernel,
        (rows4, gate_mat, up_mat),
        (pltpu.HBM((slots, model), BF16), pltpu.HBM((3 * width, slots), F32)),
        "forward",
        12,
        out_specs=[hbm(), hbm()],
        scratch=[
            pltpu.VMEM((slots, model), BF16),
            pltpu.VMEM((3 * width, slots), F32),
            pltpu.SemaphoreType.DMA((2,)),
        ],
    )
    terms, pair = call(
        backward_kernel,
        far(grads4, down_mat, full_rows, mid),
        (pltpu.HBM((3 * width, model), BF16), pltpu.HBM((2 * width, slots), BF16)),
        "backward",
        16,
        in_specs=[hbm()] * 4,
        out_specs=[hbm(), hbm()],
        scratch=[
            pltpu.VMEM((quarters, mains, packed_width), BF16),
            pltpu.VMEM((width, model), BF16),
            pltpu.VMEM((slots, model), BF16),
            pltpu.VMEM((3 * width, slots), F32),
            pltpu.VMEM((2 * width, slots), BF16),
            pltpu.VMEM((quarters, 3 * width, quarter), BF16),
            pltpu.VMEM((slots - mains, model), BF16),
            pltpu.SemaphoreType.DMA((5, quarters)),
        ],
    )
    sums = lax.psum_scatter(terms, "dp", scatter_dimension=1, tiled=True)
    partial_value = dot(pair[:width], gate_mat, TN) + dot(pair[width:], up_mat, TN)
    blocks = partial_value.astype(BF16)
    blocks = jnp.stack([blocks[:, k * quarter : (k + 1) * quarter] for k in range(quarters)])
    given = to_quarters(blocks).astype(F32)
    route_rows = (given[0] + given[1] + given[2] + given[3]).astype(BF16)
    returned = to_owners(
        jnp.concatenate(
            [
                route_rows[:mains].reshape(owners, MAIN, quarter),
                route_rows[mains:].reshape(owners, TAIL, quarter),
            ],
            axis=1,
        )
    )
    selector = (jnp.arange(slots, dtype=jnp.int32)[:, None] == slot[:1]).astype(BF16)
    token_grads = dot(selector, returned.reshape(slots, quarter), TN).astype(BF16)
    return (
        token_grads,
        sums[:width].T[None],
        sums[width : 2 * width].T[None],
        sums[2 * width :][None],
    )


def solution(mesh):
    placed = (
        P(("dp", "expert"), "fsdp"),
        P(("dp", "expert"), "fsdp"),
        P(("dp", "expert"), None),
        P(("dp", "expert"), None),
        P("expert", None, "fsdp"),
        P("expert", None, "fsdp"),
        P("expert", "fsdp", None),
    )
    return jax.shard_map(
        local,
        mesh=mesh,
        in_specs=placed,
        out_specs=(
            P(("dp", "expert"), "fsdp"),
            P("expert", "dp", "fsdp"),
            P("expert", "dp", "fsdp"),
            P("expert", "fsdp", "dp"),
        ),
        check_vma=False,
    )
```

```python
import jax
import jax.numpy as jnp
from jax import lax
from jax.experimental import pallas as pl
from jax.experimental.pallas import tpu as pltpu
from jax.sharding import PartitionSpec as P

CAP = 10
MAIN = 8
TAIL = CAP - MAIN
LATE = 16
PIECES = MAIN // TAIL
F32 = jnp.float32
BF16 = jnp.bfloat16
NN = (((1,), (0,)), ((), ()))
NT = (((1,), (1,)), ((), ()))
TN = (((0,), (0,)), ((), ()))


def dot(a, b, dims=NN):
    return lax.dot_general(a, b, dims, preferred_element_type=F32)


def iota(shape, axis):
    return lax.broadcasted_iota(jnp.int32, shape, axis)


def places(routes, owners):
    count = routes.shape[1]
    target = jnp.sum(jnp.where(routes < owners, routes, 0), axis=0, keepdims=True)
    mine = iota((owners, count), 0) == target
    earlier = (iota((count, count), 0) < iota((count, count), 1)).astype(BF16)
    before = dot(mine.astype(BF16), earlier)
    rank = jnp.sum(jnp.where(mine, before, 0.0), axis=0, keepdims=True).astype(jnp.int32)
    return target, rank


def send_kernel(
    owners, routes_hbm, gates_hbm, tokens_hbm, cotangent_hbm, out_ref, slot_ref,
    routes_ref, gates_ref, tokens_ref, cotangent_ref, sems,
):
    fetches = [
        pltpu.make_async_copy(source, near, sems.at[i])
        for i, (source, near) in enumerate(
            (
                (routes_hbm, routes_ref),
                (gates_hbm, gates_ref),
                (cotangent_hbm, cotangent_ref),
                (tokens_hbm, tokens_ref),
            )
        )
    ]
    for fetch in fetches:
        fetch.start()
    fetches[0].wait()
    routes = routes_ref[...]
    target, rank = places(routes, owners)
    slot_ref[...] = jnp.broadcast_to(target * CAP + rank, slot_ref.shape)
    fetches[1].wait()
    gate = jnp.where(routes < owners, gates_ref[...], 0.0)
    gate = jnp.sum(jnp.transpose(gate), axis=1, keepdims=True)
    fetches[2].wait()
    scaled = (gate * cotangent_ref[...].astype(F32)).astype(BF16)
    fetches[3].wait()
    values = jnp.concatenate([tokens_ref[...], scaled], axis=0)
    count, quarter = values.shape
    width = quarter // PIECES
    rows = owners * 2 * MAIN
    row, column = iota((rows, count), 0), iota((rows, count), 1)
    target = jnp.concatenate([target, target], axis=1)
    rank = jnp.concatenate([rank, rank], axis=1)
    place = row % MAIN
    wanted = (row // (2 * MAIN) == target) & (row // MAIN % 2 == column // (count // 2))
    main_pick = (wanted & (place == rank)).astype(BF16)
    out_ref[:, :quarter] = dot(main_pick, values).astype(BF16)
    in_tail = wanted & (place // PIECES + MAIN == rank)
    tail = jnp.zeros((rows, width), F32)
    for p in range(PIECES):
        pick = (in_tail & (place % PIECES == p)).astype(BF16)
        tail = tail + dot(pick, values[:, p * width : (p + 1) * width])
    out_ref[:, quarter:] = tail.astype(BF16)


def tail_pick(rows, p):
    tails = rows // MAIN * TAIL
    slot, row = iota((tails, rows), 0), iota((tails, rows), 1)
    return (row == slot // TAIL * MAIN + slot % TAIL * PIECES + p).astype(BF16)


def forward_kernel(
    rows_ref, gate_ref, up_ref, full_hbm, mid_hbm, late_hbm, late_tail_hbm,
    full_ref, mid_ref, late_ref, late_tail_ref, sems,
):
    quarters, both, _ = rows_ref.shape
    mains = both - LATE
    quarter = full_ref.shape[1] // quarters
    width = quarter // PIECES
    wide = gate_ref.shape[0]
    picks = [tail_pick(mains, p) for p in range(PIECES)]
    for j in range(quarters):
        low = j * quarter
        full_ref[:mains, low : low + quarter] = rows_ref[j, :mains, :quarter]
        packed = rows_ref[j, :mains, quarter:]
        for p in range(PIECES):
            start = low + p * width
            full_ref[mains:, start : start + width] = dot(picks[p], packed).astype(BF16)
        late_ref[:, low : low + quarter] = rows_ref[j, mains:, :quarter]
        late_tail_ref[j] = rows_ref[j, mains:, quarter:]
    keeps = [
        pltpu.make_async_copy(full_ref, full_hbm, sems.at[0]),
        pltpu.make_async_copy(late_ref, late_hbm, sems.at[1]),
        pltpu.make_async_copy(late_tail_ref, late_tail_hbm, sems.at[2]),
    ]
    for keep in keeps:
        keep.start()
    gate_pre = jnp.zeros((wide, full_ref.shape[0]), F32)
    up_pre = jnp.zeros((wide, full_ref.shape[0]), F32)
    for j in range(quarters):
        low = j * quarter
        block = full_ref[:, low : low + quarter]
        gate_pre = gate_pre + dot(gate_ref[:, low : low + quarter], block, NT)
        up_pre = up_pre + dot(up_ref[:, low : low + quarter], block, NT)
    sigmoid_gate = jax.nn.sigmoid(gate_pre)
    activated = gate_pre * sigmoid_gate
    mid_ref[:wide, :] = up_pre * sigmoid_gate * (1.0 + gate_pre * (1.0 - sigmoid_gate))
    mid_ref[wide : 2 * wide, :] = activated
    mid_ref[2 * wide :, :] = activated * up_pre
    keeps.append(pltpu.make_async_copy(mid_ref, mid_hbm, sems.at[3]))
    keeps[3].start()
    for keep in keeps:
        keep.wait()


def backward_kernel(
    grads_hbm, late_hbm, late_tail_hbm, down_hbm, full_hbm, mid_hbm, terms_hbm, pair_hbm,
    grads_ref, tail_ref, down_ref, full_ref, mid_ref, pair_ref, pairs_ref, downs_ref, sems,
):
    quarters, early, _ = grads_hbm.shape
    mains = early + LATE
    quarter = full_ref.shape[1] // quarters
    width = quarter // PIECES
    wide = down_ref.shape[0]

    def columns(ref, j):
        return ref.at[:, j * quarter : (j + 1) * quarter]

    mid_in = pltpu.make_async_copy(mid_hbm, mid_ref, sems.at[5, 0])
    tail_in = pltpu.make_async_copy(
        grads_hbm.at[:, :, quarter:], tail_ref.at[:, :early, :], sems.at[5, 1]
    )
    late_tail_in = pltpu.make_async_copy(
        late_tail_hbm, tail_ref.at[:, early:, :], sems.at[5, 2]
    )
    late_in = pltpu.make_async_copy(late_hbm, grads_ref.at[early:mains, :], sems.at[5, 3])
    grads_in = [
        pltpu.make_async_copy(
            grads_hbm.at[j, :, :quarter],
            grads_ref.at[:early, j * quarter : (j + 1) * quarter],
            sems.at[0, j],
        )
        for j in range(quarters)
    ]
    down_in = [
        pltpu.make_async_copy(columns(down_hbm, j), columns(down_ref, j), sems.at[1, j])
        for j in range(quarters)
    ]
    full_in = [
        pltpu.make_async_copy(columns(full_hbm, j), columns(full_ref, j), sems.at[2, j])
        for j in range(quarters)
    ]
    tail_in.start()
    late_tail_in.start()
    late_in.start()
    grads_in[0].start()
    down_in[0].start()
    mid_in.start()
    for j in range(1, quarters):
        grads_in[j].start()
        down_in[j].start()
    for j in range(quarters):
        full_in[j].start()
    picks = [tail_pick(mains, p) for p in range(PIECES)]
    hidden_grad = jnp.zeros((wide, grads_ref.shape[0]), F32)
    tail_in.wait()
    late_tail_in.wait()
    late_in.wait()
    outs = []
    for j in range(quarters):
        low = j * quarter
        for p in range(PIECES):
            start = low + p * width
            grads_ref[mains:, start : start + width] = dot(picks[p], tail_ref[j]).astype(BF16)
        grads_in[j].wait()
        down_in[j].wait()
        block = grads_ref[:, low : low + quarter]
        hidden_grad = hidden_grad + dot(down_ref[:, low : low + quarter], block, NT)
        if j == 0:
            mid_in.wait()
            hidden = mid_ref[2 * wide :, :].astype(BF16)
        downs_ref[j] = dot(hidden, block).astype(BF16)
        out = pltpu.make_async_copy(
            downs_ref.at[j],
            terms_hbm.at[2 * wide :, low : low + quarter],
            sems.at[3, j],
        )
        out.start()
        outs.append(out)
    pair_ref[:wide, :] = (hidden_grad * mid_ref[:wide, :]).astype(BF16)
    pair_ref[wide:, :] = (hidden_grad * mid_ref[wide : 2 * wide, :]).astype(BF16)
    out = pltpu.make_async_copy(pair_ref, pair_hbm, sems.at[6, 0])
    out.start()
    outs.append(out)
    for j in range(quarters):
        low = j * quarter
        full_in[j].wait()
        pairs_ref[j] = dot(pair_ref[...], full_ref[:, low : low + quarter]).astype(BF16)
        out = pltpu.make_async_copy(
            pairs_ref.at[j],
            terms_hbm.at[: 2 * wide, low : low + quarter],
            sems.at[4, j],
        )
        out.start()
        outs.append(out)
    for out in outs:
        out.wait()


def split_kernel(sums_hbm, *refs):
    sems = refs[-1]
    wide = sums_hbm.shape[0] // (len(refs) - 1)
    copies = [
        pltpu.make_async_copy(sums_hbm.at[i * wide : (i + 1) * wide, :], part, sems.at[i])
        for i, part in enumerate(refs[:-1])
    ]
    for copy in copies:
        copy.start()
    for copy in copies:
        copy.wait()


def vmem():
    return pl.BlockSpec(memory_space=pltpu.VMEM)


def hbm():
    return pl.BlockSpec(memory_space=pltpu.HBM)


def far(*arrays):
    return [pltpu.with_memory_space_constraint(x, pltpu.HBM) for x in arrays]


def call(kernel, operands, outs, name, limit_mib, in_specs=None, out_specs=None, scratch=()):
    return pl.pallas_call(
        kernel,
        out_shape=outs,
        in_specs=in_specs if in_specs is not None else [vmem() for _ in operands],
        out_specs=out_specs if out_specs is not None else [vmem() for _ in outs],
        scratch_shapes=scratch,
        compiler_params=pltpu.CompilerParams(vmem_limit_bytes=limit_mib * 1024 * 1024),
        name=name,
    )(*operands)


def local(tokens, cotangent, routes, route_gates, gate_weight, up_weight, down_weight):
    owners = lax.axis_size("expert")
    quarters = lax.axis_size("fsdp")
    count, quarter = tokens.shape
    model = quarter * quarters
    mains = owners * MAIN
    slots = owners * CAP
    packed_width = quarter + quarter // PIECES

    def to_owners(x):
        return lax.all_to_all(x, "expert", split_axis=0, concat_axis=0, tiled=True)

    def to_quarters(x):
        return lax.all_to_all(x, "fsdp", split_axis=0, concat_axis=0, tiled=True)

    sent, slot = call(
        lambda *refs: send_kernel(owners, *refs),
        far(routes.T, route_gates.T, tokens, cotangent),
        (
            jax.ShapeDtypeStruct((2 * mains, packed_width), BF16),
            jax.ShapeDtypeStruct((8, count), jnp.int32),
        ),
        "send",
        8,
        in_specs=[hbm()] * 4,
        scratch=[
            pltpu.VMEM(routes.shape[::-1], jnp.int32),
            pltpu.VMEM(route_gates.shape[::-1], F32),
            pltpu.VMEM(tokens.shape, BF16),
            pltpu.VMEM(cotangent.shape, BF16),
            pltpu.SemaphoreType.DMA((4,)),
        ],
    )
    received = to_owners(sent.reshape(owners, 2 * MAIN, packed_width))
    recv_rows = received[:, :MAIN].reshape(mains, packed_width)
    recv_grads = received[:, MAIN:].reshape(mains, packed_width)
    early = mains - LATE
    grads4 = lax.all_gather(recv_grads[:early], "fsdp", axis=0, tiled=True)
    grads4 = grads4.reshape(quarters, early, packed_width)
    near = jnp.concatenate([recv_rows, recv_grads[early:]], axis=0)
    rows4 = to_quarters(jnp.broadcast_to(near[None], (quarters, mains + LATE, packed_width)))
    gate_mat = jnp.swapaxes(gate_weight, 1, 2)[0]
    up_mat = jnp.swapaxes(up_weight, 1, 2)[0]
    down_mat = down_weight[0]
    width = gate_mat.shape[0]
    tail_width = packed_width - quarter
    full_rows, mid, late, late_tail = call(
        forward_kernel,
        (rows4, gate_mat, up_mat),
        (
            pltpu.HBM((slots, model), BF16),
            pltpu.HBM((3 * width, slots), F32),
            pltpu.HBM((LATE, model), BF16),
            pltpu.HBM((quarters, LATE, tail_width), BF16),
        ),
        "forward",
        12,
        out_specs=[hbm()] * 4,
        scratch=[
            pltpu.VMEM((slots, model), BF16),
            pltpu.VMEM((3 * width, slots), F32),
            pltpu.VMEM((LATE, model), BF16),
            pltpu.VMEM((quarters, LATE, tail_width), BF16),
            pltpu.SemaphoreType.DMA((4,)),
        ],
    )
    terms, pair = call(
        backward_kernel,
        far(grads4, late, late_tail, down_mat, full_rows, mid),
        (pltpu.HBM((3 * width, model), BF16), pltpu.HBM((2 * width, slots), BF16)),
        "backward",
        16,
        in_specs=[hbm()] * 6,
        out_specs=[hbm(), hbm()],
        scratch=[
            pltpu.VMEM((slots, model), BF16),
            pltpu.VMEM((quarters, mains, tail_width), BF16),
            pltpu.VMEM((width, model), BF16),
            pltpu.VMEM((slots, model), BF16),
            pltpu.VMEM((3 * width, slots), F32),
            pltpu.VMEM((2 * width, slots), BF16),
            pltpu.VMEM((quarters, 2 * width, quarter), BF16),
            pltpu.VMEM((quarters, width, quarter), BF16),
            pltpu.SemaphoreType.DMA((7, 4)),
        ],
    )
    sums = lax.psum_scatter(terms, "dp", scatter_dimension=1, tiled=True)
    partial_value = dot(pair[:width], gate_mat, TN) + dot(pair[width:], up_mat, TN)
    blocks = partial_value.astype(BF16)
    blocks = jnp.stack([blocks[:, k * quarter : (k + 1) * quarter] for k in range(quarters)])
    given = to_quarters(blocks).astype(F32)
    route_rows = (given[0] + given[1] + given[2] + given[3]).astype(BF16)
    returned = to_owners(
        jnp.concatenate(
            [
                route_rows[:mains].reshape(owners, MAIN, quarter),
                route_rows[mains:].reshape(owners, TAIL, quarter),
            ],
            axis=1,
        )
    )
    selector = (jnp.arange(slots, dtype=jnp.int32)[:, None] == slot[:1]).astype(BF16)
    token_grads = dot(selector, returned.reshape(slots, quarter), TN).astype(BF16)
    piece = pltpu.HBM((width, sums.shape[1]), BF16)
    gate_sum, up_sum, down_sum = call(
        split_kernel,
        far(sums),
        (piece, piece, piece),
        "split",
        4,
        in_specs=[hbm()],
        out_specs=[hbm()] * 3,
        scratch=[pltpu.SemaphoreType.DMA((3,))],
    )
    return token_grads, gate_sum.T[None], up_sum.T[None], down_sum[None]


def solution(mesh):
    placed = (
        P(("dp", "expert"), "fsdp"),
        P(("dp", "expert"), "fsdp"),
        P(("dp", "expert"), None),
        P(("dp", "expert"), None),
        P("expert", None, "fsdp"),
        P("expert", None, "fsdp"),
        P("expert", "fsdp", None),
    )
    return jax.shard_map(
        local,
        mesh=mesh,
        in_specs=placed,
        out_specs=(
            P(("dp", "expert"), "fsdp"),
            P("expert", "dp", "fsdp"),
            P("expert", "dp", "fsdp"),
            P("expert", "fsdp", "dp"),
        ),
        check_vma=False,
    )
```

```python
import jax
import jax.numpy as jnp
from jax import lax
from jax.experimental import pallas as pl
from jax.experimental.pallas import tpu as pltpu
from jax.sharding import PartitionSpec as P

CAP = 10
MAIN = 8
TAIL = CAP - MAIN
PIECES = MAIN // TAIL
F32 = jnp.float32
BF16 = jnp.bfloat16
NN = (((1,), (0,)), ((), ()))
NT = (((1,), (1,)), ((), ()))
TN = (((0,), (0,)), ((), ()))


def dot(a, b, dims=NN):
    return lax.dot_general(a, b, dims, preferred_element_type=F32)


def iota(shape, axis):
    return lax.broadcasted_iota(jnp.int32, shape, axis)


def places(routes, owners):
    count = routes.shape[1]
    target = jnp.sum(jnp.where(routes < owners, routes, 0), axis=0, keepdims=True)
    mine = iota((owners, count), 0) == target
    earlier = (iota((count, count), 0) < iota((count, count), 1)).astype(BF16)
    before = dot(mine.astype(BF16), earlier)
    rank = jnp.sum(jnp.where(mine, before, 0.0), axis=0, keepdims=True).astype(jnp.int32)
    return target, rank


def send_kernel(
    owners, routes_hbm, gates_hbm, tokens_hbm, cotangent_hbm, out_ref, slot_ref,
    routes_ref, gates_ref, tokens_ref, cotangent_ref, sems,
):
    fetches = [
        pltpu.make_async_copy(source, near, sems.at[i])
        for i, (source, near) in enumerate(
            (
                (routes_hbm, routes_ref),
                (gates_hbm, gates_ref),
                (cotangent_hbm, cotangent_ref),
                (tokens_hbm, tokens_ref),
            )
        )
    ]
    for fetch in fetches:
        fetch.start()
    fetches[0].wait()
    routes = routes_ref[...]
    target, rank = places(routes, owners)
    slot_ref[...] = jnp.broadcast_to(target * CAP + rank, slot_ref.shape)
    fetches[1].wait()
    gate = jnp.where(routes < owners, gates_ref[...], 0.0)
    gate = jnp.sum(jnp.transpose(gate), axis=1, keepdims=True)
    fetches[2].wait()
    scaled = (gate * cotangent_ref[...].astype(F32)).astype(BF16)
    fetches[3].wait()
    values = jnp.concatenate([tokens_ref[...], scaled], axis=0)
    count, quarter = values.shape
    width = quarter // PIECES
    rows = owners * 2 * MAIN
    row, column = iota((rows, count), 0), iota((rows, count), 1)
    target = jnp.concatenate([target, target], axis=1)
    rank = jnp.concatenate([rank, rank], axis=1)
    place = row % MAIN
    wanted = (row // (2 * MAIN) == target) & (row // MAIN % 2 == column // (count // 2))
    main_pick = (wanted & (place == rank)).astype(BF16)
    out_ref[:, :quarter] = dot(main_pick, values).astype(BF16)
    in_tail = wanted & (place // PIECES + MAIN == rank)
    tail = jnp.zeros((rows, width), F32)
    for p in range(PIECES):
        pick = (in_tail & (place % PIECES == p)).astype(BF16)
        tail = tail + dot(pick, values[:, p * width : (p + 1) * width])
    out_ref[:, quarter:] = tail.astype(BF16)


def tail_pick(rows, p):
    tails = rows // MAIN * TAIL
    slot, row = iota((tails, rows), 0), iota((tails, rows), 1)
    return (row == slot // TAIL * MAIN + slot % TAIL * PIECES + p).astype(BF16)


def forward_kernel(
    rows_ref, gate_ref, up_ref, full_hbm, mid_hbm, full_ref, mid_ref, sems
):
    quarters, mains, _ = rows_ref.shape
    quarter = full_ref.shape[1] // quarters
    width = quarter // PIECES
    wide = gate_ref.shape[0]
    picks = [tail_pick(mains, p) for p in range(PIECES)]
    for j in range(quarters):
        low = j * quarter
        full_ref[:mains, low : low + quarter] = rows_ref[j, :, :quarter]
        packed = rows_ref[j, :, quarter:]
        for p in range(PIECES):
            start = low + p * width
            full_ref[mains:, start : start + width] = dot(picks[p], packed).astype(BF16)
    keep_full = pltpu.make_async_copy(full_ref, full_hbm, sems.at[0])
    keep_full.start()
    gate_pre = jnp.zeros((wide, full_ref.shape[0]), F32)
    up_pre = jnp.zeros((wide, full_ref.shape[0]), F32)
    for j in range(quarters):
        low = j * quarter
        block = full_ref[:, low : low + quarter]
        gate_pre = gate_pre + dot(gate_ref[:, low : low + quarter], block, NT)
        up_pre = up_pre + dot(up_ref[:, low : low + quarter], block, NT)
    sigmoid_gate = jax.nn.sigmoid(gate_pre)
    activated = gate_pre * sigmoid_gate
    mid_ref[:wide, :] = up_pre * sigmoid_gate * (1.0 + gate_pre * (1.0 - sigmoid_gate))
    mid_ref[wide : 2 * wide, :] = activated
    mid_ref[2 * wide :, :] = activated * up_pre
    keep_mid = pltpu.make_async_copy(mid_ref, mid_hbm, sems.at[1])
    keep_mid.start()
    keep_full.wait()
    keep_mid.wait()


def backward_kernel(
    grads_hbm, down_hbm, full_hbm, mid_hbm, terms_hbm, pair_hbm,
    grads_ref, tail_ref, down_ref, full_ref, mid_ref, pair_ref, pairs_ref, downs_ref, sems,
):
    quarters, mains, _ = grads_hbm.shape
    quarter = full_ref.shape[1] // quarters
    width = quarter // PIECES
    wide = down_ref.shape[0]

    def columns(ref, j):
        return ref.at[:, j * quarter : (j + 1) * quarter]

    mid_in = pltpu.make_async_copy(mid_hbm, mid_ref, sems.at[5, 0])
    tail_in = pltpu.make_async_copy(grads_hbm.at[:, :, quarter:], tail_ref, sems.at[5, 1])
    grads_in = [
        pltpu.make_async_copy(
            grads_hbm.at[j, :, :quarter],
            grads_ref.at[:mains, j * quarter : (j + 1) * quarter],
            sems.at[0, j],
        )
        for j in range(quarters)
    ]
    down_in = [
        pltpu.make_async_copy(columns(down_hbm, j), columns(down_ref, j), sems.at[1, j])
        for j in range(quarters)
    ]
    full_in = [
        pltpu.make_async_copy(columns(full_hbm, j), columns(full_ref, j), sems.at[2, j])
        for j in range(quarters)
    ]
    tail_in.start()
    grads_in[0].start()
    down_in[0].start()
    mid_in.start()
    for j in range(1, quarters):
        grads_in[j].start()
        down_in[j].start()
    for j in range(quarters):
        full_in[j].start()
    picks = [tail_pick(mains, p) for p in range(PIECES)]
    hidden_grad = jnp.zeros((wide, grads_ref.shape[0]), F32)
    tail_in.wait()
    outs = []
    for j in range(quarters):
        low = j * quarter
        for p in range(PIECES):
            start = low + p * width
            grads_ref[mains:, start : start + width] = dot(picks[p], tail_ref[j]).astype(BF16)
        grads_in[j].wait()
        down_in[j].wait()
        block = grads_ref[:, low : low + quarter]
        hidden_grad = hidden_grad + dot(down_ref[:, low : low + quarter], block, NT)
        if j == 0:
            mid_in.wait()
            hidden = mid_ref[2 * wide :, :].astype(BF16)
        downs_ref[j] = dot(hidden, block).astype(BF16)
        out = pltpu.make_async_copy(
            downs_ref.at[j],
            terms_hbm.at[2 * wide :, low : low + quarter],
            sems.at[3, j],
        )
        out.start()
        outs.append(out)
    pair_ref[:wide, :] = (hidden_grad * mid_ref[:wide, :]).astype(BF16)
    pair_ref[wide:, :] = (hidden_grad * mid_ref[wide : 2 * wide, :]).astype(BF16)
    out = pltpu.make_async_copy(pair_ref, pair_hbm, sems.at[6, 0])
    out.start()
    outs.append(out)
    for j in range(quarters):
        low = j * quarter
        full_in[j].wait()
        pairs_ref[j] = dot(pair_ref[...], full_ref[:, low : low + quarter]).astype(BF16)
        out = pltpu.make_async_copy(
            pairs_ref.at[j],
            terms_hbm.at[: 2 * wide, low : low + quarter],
            sems.at[4, j],
        )
        out.start()
        outs.append(out)
    for out in outs:
        out.wait()


def split_kernel(sums_hbm, *refs):
    *parts, near_ref, sems = refs
    wide = sums_hbm.shape[0] // len(parts)
    loads, stores = [], []
    for i, part in enumerate(parts):
        block = near_ref.at[i * wide : (i + 1) * wide, :]
        loads.append(
            pltpu.make_async_copy(sums_hbm.at[i * wide : (i + 1) * wide, :], block, sems.at[0, i])
        )
        stores.append(pltpu.make_async_copy(block, part, sems.at[1, i]))
    for load in loads:
        load.start()
    for load, store in zip(loads, stores):
        load.wait()
        store.start()
    for store in stores:
        store.wait()


def vmem():
    return pl.BlockSpec(memory_space=pltpu.VMEM)


def hbm():
    return pl.BlockSpec(memory_space=pltpu.HBM)


def far(*arrays):
    return [pltpu.with_memory_space_constraint(x, pltpu.HBM) for x in arrays]


def call(kernel, operands, outs, name, limit_mib, in_specs=None, out_specs=None, scratch=()):
    return pl.pallas_call(
        kernel,
        out_shape=outs,
        in_specs=in_specs if in_specs is not None else [vmem() for _ in operands],
        out_specs=out_specs if out_specs is not None else [vmem() for _ in outs],
        scratch_shapes=scratch,
        compiler_params=pltpu.CompilerParams(vmem_limit_bytes=limit_mib * 1024 * 1024),
        name=name,
    )(*operands)


def local(tokens, cotangent, routes, route_gates, gate_weight, up_weight, down_weight):
    owners = lax.axis_size("expert")
    quarters = lax.axis_size("fsdp")
    count, quarter = tokens.shape
    model = quarter * quarters
    mains = owners * MAIN
    slots = owners * CAP
    packed_width = quarter + quarter // PIECES

    def to_owners(x):
        return lax.all_to_all(x, "expert", split_axis=0, concat_axis=0, tiled=True)

    def to_quarters(x):
        return lax.all_to_all(x, "fsdp", split_axis=0, concat_axis=0, tiled=True)

    sent, slot = call(
        lambda *refs: send_kernel(owners, *refs),
        far(routes.T, route_gates.T, tokens, cotangent),
        (
            jax.ShapeDtypeStruct((2 * mains, packed_width), BF16),
            jax.ShapeDtypeStruct((8, count), jnp.int32),
        ),
        "send",
        8,
        in_specs=[hbm()] * 4,
        scratch=[
            pltpu.VMEM(routes.shape[::-1], jnp.int32),
            pltpu.VMEM(route_gates.shape[::-1], F32),
            pltpu.VMEM(tokens.shape, BF16),
            pltpu.VMEM(cotangent.shape, BF16),
            pltpu.SemaphoreType.DMA((4,)),
        ],
    )
    received = to_owners(sent.reshape(owners, 2 * MAIN, packed_width))
    recv_rows = received[:, :MAIN].reshape(mains, packed_width)
    recv_grads = received[:, MAIN:].reshape(mains, packed_width)
    grads4 = lax.all_gather(recv_grads, "fsdp", axis=0, tiled=True)
    grads4 = grads4.reshape(quarters, mains, packed_width)
    rows4 = to_quarters(jnp.broadcast_to(recv_rows[None], (quarters, mains, packed_width)))
    gate_mat = jnp.swapaxes(gate_weight, 1, 2)[0]
    up_mat = jnp.swapaxes(up_weight, 1, 2)[0]
    down_mat = down_weight[0]
    width = gate_mat.shape[0]
    tail_width = packed_width - quarter
    full_rows, mid = call(
        forward_kernel,
        (rows4, gate_mat, up_mat),
        (
            pltpu.HBM((slots, model), BF16),
            pltpu.HBM((3 * width, slots), F32),
        ),
        "forward",
        12,
        out_specs=[hbm()] * 2,
        scratch=[
            pltpu.VMEM((slots, model), BF16),
            pltpu.VMEM((3 * width, slots), F32),
            pltpu.SemaphoreType.DMA((2,)),
        ],
    )
    terms, pair = call(
        backward_kernel,
        far(grads4, down_mat, full_rows, mid),
        (pltpu.HBM((3 * width, model), BF16), pltpu.HBM((2 * width, slots), BF16)),
        "backward",
        16,
        in_specs=[hbm()] * 4,
        out_specs=[hbm(), hbm()],
        scratch=[
            pltpu.VMEM((slots, model), BF16),
            pltpu.VMEM((quarters, mains, tail_width), BF16),
            pltpu.VMEM((width, model), BF16),
            pltpu.VMEM((slots, model), BF16),
            pltpu.VMEM((3 * width, slots), F32),
            pltpu.VMEM((2 * width, slots), BF16),
            pltpu.VMEM((quarters, 2 * width, quarter), BF16),
            pltpu.VMEM((quarters, width, quarter), BF16),
            pltpu.SemaphoreType.DMA((7, 4)),
        ],
    )
    sums = lax.psum_scatter(terms, "dp", scatter_dimension=1, tiled=True)
    partial_value = dot(pair[:width], gate_mat, TN) + dot(pair[width:], up_mat, TN)
    blocks = partial_value.astype(BF16)
    blocks = jnp.stack([blocks[:, k * quarter : (k + 1) * quarter] for k in range(quarters)])
    given = to_quarters(blocks).astype(F32)
    route_rows = (given[0] + given[1] + given[2] + given[3]).astype(BF16)
    returned = to_owners(
        jnp.concatenate(
            [
                route_rows[:mains].reshape(owners, MAIN, quarter),
                route_rows[mains:].reshape(owners, TAIL, quarter),
            ],
            axis=1,
        )
    )
    selector = (jnp.arange(slots, dtype=jnp.int32)[:, None] == slot[:1]).astype(BF16)
    token_grads = dot(selector, returned.reshape(slots, quarter), TN).astype(BF16)
    piece = pltpu.HBM((width, sums.shape[1]), BF16)
    gate_sum, up_sum, down_sum = call(
        split_kernel,
        far(sums),
        (piece, piece, piece),
        "split",
        4,
        in_specs=[hbm()],
        out_specs=[hbm()] * 3,
        scratch=[pltpu.VMEM(sums.shape, BF16), pltpu.SemaphoreType.DMA((2, 3))],
    )
    return token_grads, gate_sum.T[None], up_sum.T[None], down_sum[None]


def solution(mesh):
    placed = (
        P(("dp", "expert"), "fsdp"),
        P(("dp", "expert"), "fsdp"),
        P(("dp", "expert"), None),
        P(("dp", "expert"), None),
        P("expert", None, "fsdp"),
        P("expert", None, "fsdp"),
        P("expert", "fsdp", None),
    )
    return jax.shard_map(
        local,
        mesh=mesh,
        in_specs=placed,
        out_specs=(
            P(("dp", "expert"), "fsdp"),
            P("expert", "dp", "fsdp"),
            P("expert", "dp", "fsdp"),
            P("expert", "fsdp", "dp"),
        ),
        check_vma=False,
    )
```

```python
import jax
import jax.numpy as jnp
from jax import lax
from jax.experimental import pallas as pl
from jax.experimental.pallas import tpu as pltpu
from jax.sharding import PartitionSpec as P

CAP = 10
MAIN = 8
TAIL = CAP - MAIN
PIECES = MAIN // TAIL
F32 = jnp.float32
BF16 = jnp.bfloat16
NN = (((1,), (0,)), ((), ()))
NT = (((1,), (1,)), ((), ()))
TN = (((0,), (0,)), ((), ()))


def dot(a, b, dims=NN):
    return lax.dot_general(a, b, dims, preferred_element_type=F32)


def iota(shape, axis):
    return lax.broadcasted_iota(jnp.int32, shape, axis)


def places(routes, owners):
    count = routes.shape[1]
    target = jnp.sum(jnp.where(routes < owners, routes, 0), axis=0, keepdims=True)
    mine = iota((owners, count), 0) == target
    earlier = (iota((count, count), 0) < iota((count, count), 1)).astype(BF16)
    before = dot(mine.astype(BF16), earlier)
    rank = jnp.sum(jnp.where(mine, before, 0.0), axis=0, keepdims=True).astype(jnp.int32)
    return target, rank


def send_kernel(
    owners, routes_hbm, gates_hbm, tokens_hbm, cotangent_hbm, out_ref, slot_ref,
    routes_ref, gates_ref, tokens_ref, cotangent_ref, sems,
):
    fetches = [
        pltpu.make_async_copy(source, near, sems.at[i])
        for i, (source, near) in enumerate(
            (
                (routes_hbm, routes_ref),
                (gates_hbm, gates_ref),
                (cotangent_hbm, cotangent_ref),
                (tokens_hbm, tokens_ref),
            )
        )
    ]
    for fetch in fetches:
        fetch.start()
    fetches[0].wait()
    routes = routes_ref[...]
    target, rank = places(routes, owners)
    slot_ref[...] = jnp.broadcast_to(target * CAP + rank, slot_ref.shape)
    fetches[1].wait()
    gate = jnp.where(routes < owners, gates_ref[...], 0.0)
    gate = jnp.sum(jnp.transpose(gate), axis=1, keepdims=True)
    fetches[2].wait()
    scaled = (gate * cotangent_ref[...].astype(F32)).astype(BF16)
    fetches[3].wait()
    values = jnp.concatenate([tokens_ref[...], scaled], axis=0)
    count, quarter = values.shape
    width = quarter // PIECES
    rows = owners * 2 * MAIN
    row, column = iota((rows, count), 0), iota((rows, count), 1)
    target = jnp.concatenate([target, target], axis=1)
    rank = jnp.concatenate([rank, rank], axis=1)
    place = row % MAIN
    wanted = (row // (2 * MAIN) == target) & (row // MAIN % 2 == column // (count // 2))
    main_pick = (wanted & (place == rank)).astype(BF16)
    out_ref[:, :quarter] = dot(main_pick, values).astype(BF16)
    in_tail = wanted & (place // PIECES + MAIN == rank)
    tail = jnp.zeros((rows, width), F32)
    for p in range(PIECES):
        pick = (in_tail & (place % PIECES == p)).astype(BF16)
        tail = tail + dot(pick, values[:, p * width : (p + 1) * width])
    out_ref[:, quarter:] = tail.astype(BF16)


def tail_pick(rows):
    tails = rows // MAIN * TAIL
    out, row = iota((tails * PIECES, rows), 0), iota((tails * PIECES, rows), 1)
    slot, piece = out % tails, out // tails
    return (row == slot // TAIL * MAIN + slot % TAIL * PIECES + piece).astype(BF16)


def unpack_tail(pick, packed, ref, mains, low):
    tails, width = ref.shape[0] - mains, packed.shape[1]
    pieces = dot(pick, packed).astype(BF16)
    for p in range(PIECES):
        start = low + p * width
        ref[mains:, start : start + width] = pieces[p * tails : (p + 1) * tails]


def forward_kernel(
    rows_ref, gate_ref, up_ref, full_hbm, mid_hbm, full_ref, mid_ref, sems
):
    quarters, mains, _ = rows_ref.shape
    quarter = full_ref.shape[1] // quarters
    wide = gate_ref.shape[0]
    pick = tail_pick(mains)
    for j in range(quarters):
        low = j * quarter
        full_ref[:mains, low : low + quarter] = rows_ref[j, :, :quarter]
        unpack_tail(pick, rows_ref[j, :, quarter:], full_ref, mains, low)
    keep_full = pltpu.make_async_copy(full_ref, full_hbm, sems.at[0])
    keep_full.start()
    gate_pre = jnp.zeros((wide, full_ref.shape[0]), F32)
    up_pre = jnp.zeros((wide, full_ref.shape[0]), F32)
    for j in range(quarters):
        low = j * quarter
        block = full_ref[:, low : low + quarter]
        gate_pre = gate_pre + dot(gate_ref[:, low : low + quarter], block, NT)
        up_pre = up_pre + dot(up_ref[:, low : low + quarter], block, NT)
    sigmoid_gate = jax.nn.sigmoid(gate_pre)
    activated = gate_pre * sigmoid_gate
    mid_ref[:wide, :] = up_pre * sigmoid_gate * (1.0 + gate_pre * (1.0 - sigmoid_gate))
    mid_ref[wide : 2 * wide, :] = activated
    mid_ref[2 * wide :, :] = activated * up_pre
    keep_mid = pltpu.make_async_copy(mid_ref, mid_hbm, sems.at[1])
    keep_mid.start()
    keep_full.wait()
    keep_mid.wait()


def backward_kernel(
    grads_hbm, down_hbm, full_hbm, mid_hbm, terms_hbm, pair_hbm,
    grads_ref, tail_ref, down_ref, full_ref, mid_ref, pair_ref, pairs_ref, downs_ref, sems,
):
    quarters, mains, _ = grads_hbm.shape
    quarter = full_ref.shape[1] // quarters
    wide = down_ref.shape[0]

    def columns(ref, j):
        return ref.at[:, j * quarter : (j + 1) * quarter]

    mid_in = pltpu.make_async_copy(mid_hbm, mid_ref, sems.at[5, 0])
    tail_in = pltpu.make_async_copy(grads_hbm.at[:, :, quarter:], tail_ref, sems.at[5, 1])
    grads_in = [
        pltpu.make_async_copy(
            grads_hbm.at[j, :, :quarter],
            grads_ref.at[:mains, j * quarter : (j + 1) * quarter],
            sems.at[0, j],
        )
        for j in range(quarters)
    ]
    down_in = [
        pltpu.make_async_copy(columns(down_hbm, j), columns(down_ref, j), sems.at[1, j])
        for j in range(quarters)
    ]
    full_in = [
        pltpu.make_async_copy(columns(full_hbm, j), columns(full_ref, j), sems.at[2, j])
        for j in range(quarters)
    ]
    tail_in.start()
    grads_in[0].start()
    down_in[0].start()
    mid_in.start()
    for j in range(1, quarters):
        grads_in[j].start()
        down_in[j].start()
    for j in range(quarters):
        full_in[j].start()
    pick = tail_pick(mains)
    hidden_grad = jnp.zeros((wide, grads_ref.shape[0]), F32)
    tail_in.wait()
    outs = []
    for j in range(quarters):
        low = j * quarter
        unpack_tail(pick, tail_ref[j], grads_ref, mains, low)
        grads_in[j].wait()
        down_in[j].wait()
        block = grads_ref[:, low : low + quarter]
        hidden_grad = hidden_grad + dot(down_ref[:, low : low + quarter], block, NT)
        if j == 0:
            mid_in.wait()
            hidden = mid_ref[2 * wide :, :].astype(BF16)
        downs_ref[j] = dot(hidden, block).astype(BF16)
        out = pltpu.make_async_copy(
            downs_ref.at[j],
            terms_hbm.at[2 * wide :, low : low + quarter],
            sems.at[3, j],
        )
        out.start()
        outs.append(out)
    pair_ref[:wide, :] = (hidden_grad * mid_ref[:wide, :]).astype(BF16)
    pair_ref[wide:, :] = (hidden_grad * mid_ref[wide : 2 * wide, :]).astype(BF16)
    out = pltpu.make_async_copy(pair_ref, pair_hbm, sems.at[6, 0])
    out.start()
    outs.append(out)
    for j in range(quarters):
        low = j * quarter
        full_in[j].wait()
        pairs_ref[j] = dot(pair_ref[...], full_ref[:, low : low + quarter]).astype(BF16)
        out = pltpu.make_async_copy(
            pairs_ref.at[j],
            terms_hbm.at[: 2 * wide, low : low + quarter],
            sems.at[4, j],
        )
        out.start()
        outs.append(out)
    for out in outs:
        out.wait()


def split_kernel(sums_hbm, *refs):
    *parts, near_ref, sems = refs
    wide = sums_hbm.shape[0] // len(parts)
    loads, stores = [], []
    for i, part in enumerate(parts):
        block = near_ref.at[i * wide : (i + 1) * wide, :]
        loads.append(
            pltpu.make_async_copy(sums_hbm.at[i * wide : (i + 1) * wide, :], block, sems.at[0, i])
        )
        stores.append(pltpu.make_async_copy(block, part, sems.at[1, i]))
    for load in loads:
        load.start()
    for load, store in zip(loads, stores):
        load.wait()
        store.start()
    for store in stores:
        store.wait()


def vmem():
    return pl.BlockSpec(memory_space=pltpu.VMEM)


def hbm():
    return pl.BlockSpec(memory_space=pltpu.HBM)


def far(*arrays):
    return [pltpu.with_memory_space_constraint(x, pltpu.HBM) for x in arrays]


def call(kernel, operands, outs, name, limit_mib, in_specs=None, out_specs=None, scratch=()):
    return pl.pallas_call(
        kernel,
        out_shape=outs,
        in_specs=in_specs if in_specs is not None else [vmem() for _ in operands],
        out_specs=out_specs if out_specs is not None else [vmem() for _ in outs],
        scratch_shapes=scratch,
        compiler_params=pltpu.CompilerParams(vmem_limit_bytes=limit_mib * 1024 * 1024),
        name=name,
    )(*operands)


def local(tokens, cotangent, routes, route_gates, gate_weight, up_weight, down_weight):
    owners = lax.axis_size("expert")
    quarters = lax.axis_size("fsdp")
    count, quarter = tokens.shape
    model = quarter * quarters
    mains = owners * MAIN
    slots = owners * CAP
    packed_width = quarter + quarter // PIECES

    def to_owners(x):
        return lax.all_to_all(x, "expert", split_axis=0, concat_axis=0, tiled=True)

    def to_quarters(x):
        return lax.all_to_all(x, "fsdp", split_axis=0, concat_axis=0, tiled=True)

    sent, slot = call(
        lambda *refs: send_kernel(owners, *refs),
        far(routes.T, route_gates.T, tokens, cotangent),
        (
            jax.ShapeDtypeStruct((2 * mains, packed_width), BF16),
            jax.ShapeDtypeStruct((8, count), jnp.int32),
        ),
        "send",
        8,
        in_specs=[hbm()] * 4,
        scratch=[
            pltpu.VMEM(routes.shape[::-1], jnp.int32),
            pltpu.VMEM(route_gates.shape[::-1], F32),
            pltpu.VMEM(tokens.shape, BF16),
            pltpu.VMEM(cotangent.shape, BF16),
            pltpu.SemaphoreType.DMA((4,)),
        ],
    )
    received = to_owners(sent.reshape(owners, 2 * MAIN, packed_width))
    recv_rows = received[:, :MAIN].reshape(mains, packed_width)
    recv_grads = received[:, MAIN:].reshape(mains, packed_width)
    grads4 = lax.all_gather(recv_grads, "fsdp", axis=0, tiled=True)
    grads4 = grads4.reshape(quarters, mains, packed_width)
    rows4 = to_quarters(jnp.broadcast_to(recv_rows[None], (quarters, mains, packed_width)))
    gate_mat = jnp.swapaxes(gate_weight, 1, 2)[0]
    up_mat = jnp.swapaxes(up_weight, 1, 2)[0]
    down_mat = down_weight[0]
    width = gate_mat.shape[0]
    tail_width = packed_width - quarter
    full_rows, mid = call(
        forward_kernel,
        (rows4, gate_mat, up_mat),
        (
            pltpu.HBM((slots, model), BF16),
            pltpu.HBM((3 * width, slots), F32),
        ),
        "forward",
        12,
        out_specs=[hbm()] * 2,
        scratch=[
            pltpu.VMEM((slots, model), BF16),
            pltpu.VMEM((3 * width, slots), F32),
            pltpu.SemaphoreType.DMA((2,)),
        ],
    )
    terms, pair = call(
        backward_kernel,
        far(grads4, down_mat, full_rows, mid),
        (pltpu.HBM((3 * width, model), BF16), pltpu.HBM((2 * width, slots), BF16)),
        "backward",
        16,
        in_specs=[hbm()] * 4,
        out_specs=[hbm(), hbm()],
        scratch=[
            pltpu.VMEM((slots, model), BF16),
            pltpu.VMEM((quarters, mains, tail_width), BF16),
            pltpu.VMEM((width, model), BF16),
            pltpu.VMEM((slots, model), BF16),
            pltpu.VMEM((3 * width, slots), F32),
            pltpu.VMEM((2 * width, slots), BF16),
            pltpu.VMEM((quarters, 2 * width, quarter), BF16),
            pltpu.VMEM((quarters, width, quarter), BF16),
            pltpu.SemaphoreType.DMA((7, 4)),
        ],
    )
    sums = lax.psum_scatter(terms, "dp", scatter_dimension=1, tiled=True)
    partial_value = dot(pair[:width], gate_mat, TN) + dot(pair[width:], up_mat, TN)
    blocks = partial_value.astype(BF16)
    blocks = jnp.stack([blocks[:, k * quarter : (k + 1) * quarter] for k in range(quarters)])
    given = to_quarters(blocks).astype(F32)
    route_rows = (given[0] + given[1] + given[2] + given[3]).astype(BF16)
    returned = to_owners(
        jnp.concatenate(
            [
                route_rows[:mains].reshape(owners, MAIN, quarter),
                route_rows[mains:].reshape(owners, TAIL, quarter),
            ],
            axis=1,
        )
    )
    selector = (jnp.arange(slots, dtype=jnp.int32)[:, None] == slot[:1]).astype(BF16)
    token_grads = dot(selector, returned.reshape(slots, quarter), TN).astype(BF16)
    piece = pltpu.HBM((width, sums.shape[1]), BF16)
    gate_sum, up_sum, down_sum = call(
        split_kernel,
        far(sums),
        (piece, piece, piece),
        "split",
        4,
        in_specs=[hbm()],
        out_specs=[hbm()] * 3,
        scratch=[pltpu.VMEM(sums.shape, BF16), pltpu.SemaphoreType.DMA((2, 3))],
    )
    return token_grads, gate_sum.T[None], up_sum.T[None], down_sum[None]


def solution(mesh):
    placed = (
        P(("dp", "expert"), "fsdp"),
        P(("dp", "expert"), "fsdp"),
        P(("dp", "expert"), None),
        P(("dp", "expert"), None),
        P("expert", None, "fsdp"),
        P("expert", None, "fsdp"),
        P("expert", "fsdp", None),
    )
    return jax.shard_map(
        local,
        mesh=mesh,
        in_specs=placed,
        out_specs=(
            P(("dp", "expert"), "fsdp"),
            P("expert", "dp", "fsdp"),
            P("expert", "dp", "fsdp"),
            P("expert", "fsdp", "dp"),
        ),
        check_vma=False,
    )
```
